32 devices in a mesh: enc: 8 (over y, x, core), dec: 4 (over z).
Axes of the slice: x: 2, y: 2, z: 4, core: 2. Of those that a mesh axis runs over, the one named last changes fastest.
Arguments:
- queries: bfloat16 [2048, 4096], P('dec', 'enc'), may hold values from -16 to 16
- out_grad: bfloat16 [2048, 4096], P('dec', 'enc'), may hold values from -6 to 6
- memory_keys: bfloat16 [4096, 4096], P('enc'), may hold values from -6 to 6
- memory_values: bfloat16 [4096, 4096], P('enc'), may hold values from -6 to 6
- ref_blocks: int32 [2048, 8], P('dec'), may hold values from 0 to 31, as said below
- ref_counts: int32 [2048], P('dec'), may hold values from 1 to 8
Outputs:
- context: bfloat16 [2048, 4096], P('dec', 'enc')
- query_grad: bfloat16 [2048, 4096], P('dec', 'enc')
- key_grad: bfloat16 [4096, 4096], P('enc', 'dec')
- value_grad: bfloat16 [4096, 4096], P('enc', 'dec')
The draws below stay inside these ranges and needn't reach their ends.
Inputs may be any that keep to these rules, and one draw needn't show every extreme that they name: `ref_blocks`: each row holds 8 different block numbers.
All inputs are finite; a program needn't handle non-finite values.
Results may differ from the reference program's by a relative error of at most 0.0092.
Values may be sent and summed in bfloat16 or wider, within the bound.
A program may use at most 192 MiB of HBM per device.

```python
import jax
import jax.numpy as jnp
from jax import lax

HEADS = 64
DH = 64
D = 4096
BLOCK = 128
REFS = 8
TOK_DEV = 512
CELLS = 4096
BLOCKS = 32
TOKENS = 2048


def sheet_refs(key):
    sub_key = jax.random.fold_in(key, 7)
    random_part = jax.random.randint(sub_key, (TOKENS, BLOCKS), 0, 1024)
    columns = jnp.arange(BLOCKS, dtype=jnp.int32)
    weights = 10 + 20 * columns // BLOCKS
    scores = random_part * weights[None, :] * BLOCKS + columns[None, :]
    return lax.top_k(scores, REFS)[1].astype(jnp.int32)


def sheet_keys(key):
    sub_key = jax.random.fold_in(key, 3)
    base = jnp.clip(jax.random.normal(sub_key, (CELLS, D), jnp.float32), -4.0, 4.0)
    rising = 0.8 + 0.6 * jnp.arange(CELLS, dtype=jnp.float32) / CELLS
    memory = base * rising[:, None]
    return memory


def draw_memory_keys(key, part):
    return sheet_keys(key).astype(jnp.bfloat16)


def draw_queries(key, part):
    sub_key = jax.random.fold_in(key, 5)
    base = 0.125 * jnp.clip(jax.random.normal(sub_key, (TOKENS, D), jnp.float32), -4.0, 4.0)
    return base.astype(jnp.bfloat16)


def draw_ref_blocks(key, part):
    return sheet_refs(key)


def with_ends(values, own_key, low, high):
    longest = values.shape.index(max(values.shape))
    spots = []
    for shift in (0, 1):
        where = [jax.random.randint(jax.random.fold_in(own_key, axis), (), 0, length) for axis, length in enumerate(values.shape)]
        where[longest] = (where[longest] + shift) % values.shape[longest]
        spots.append(tuple(where))
    return values.at[spots[0]].set(low).at[spots[1]].set(high)


def block_levels(own_key, dims, split, low, high):
    def one(dim, parts):
        draws = jax.random.uniform(jax.random.fold_in(jax.random.fold_in(own_key, 6), dim), (parts,), jnp.float32, low / len(split), high / len(split))
        return jnp.repeat(jnp.exp(draws), dims[dim] // parts).reshape((-1,) + (1,) * (len(dims) - dim - 1))

    loudness = one(*split[0])
    for cut in split[1:]:
        loudness = loudness * one(*cut)
    return loudness


def gaussian(own_key, extent, deviation, most, pieces=(), kind=jnp.bfloat16):
    result = jax.random.normal(own_key, extent, jnp.float32) * deviation
    if len(pieces) > 0:
        result = block_levels(own_key, extent, pieces, -0.22, 0.18) * result
    return jnp.clip(result, min=-most, max=most).astype(kind)


def setup_inputs(seed: int = 0) -> dict:
    streams_of = jax.random.split(jax.random.key(seed), 7)
    queries = draw_queries(jax.random.fold_in(streams_of[6], 71), 0)
    out_grad = gaussian(streams_of[1], (TOKENS, D), 1.0, 6.0, ((0, 4), (1, 8)))
    memory_keys = draw_memory_keys(jax.random.fold_in(streams_of[6], 71), 0)
    memory_values = gaussian(streams_of[3], (CELLS, D), 1.0, 6.0, ((0, 8),))
    ref_blocks = draw_ref_blocks(jax.random.fold_in(streams_of[6], 71), 0)
    ref_counts = with_ends(jax.random.randint(streams_of[5], (TOKENS,), 1, REFS + 1), jax.random.fold_in(streams_of[5], 1), 1, REFS).astype(jnp.int32)
    return {"queries": queries, "out_grad": out_grad, "memory_keys": memory_keys, "memory_values": memory_values, "ref_blocks": ref_blocks, "ref_counts": ref_counts}


NEGATIVE = -1e30


def reference(queries, out_grad, memory_keys, memory_values, ref_blocks, ref_counts):
    token_count = queries.shape[0]
    cell_count = memory_keys.shape[0]
    block_count = cell_count // BLOCK
    head_queries = queries.reshape(token_count, HEADS, DH).transpose(1, 0, 2)
    head_grads = out_grad.reshape(token_count, HEADS, DH).transpose(1, 0, 2)
    head_keys = memory_keys.reshape(block_count, BLOCK, HEADS, DH).transpose(2, 0, 1, 3)
    head_values = memory_values.reshape(block_count, BLOCK, HEADS, DH).transpose(2, 0, 1, 3)
    live_slot = jnp.arange(REFS, dtype=jnp.int32)[None, :] < ref_counts[:, None]
    block_rows = TOK_DEV
    row_blocks = token_count // block_rows
    refs_split = ref_blocks.reshape(row_blocks, block_rows, REFS)
    live_split = live_slot.reshape(row_blocks, block_rows, REFS)

    def one_head(carry, head_data):
        query_head, grad_head, key_head, value_head = head_data
        query_split = query_head.reshape(row_blocks, block_rows, DH)
        grad_split = grad_head.reshape(row_blocks, block_rows, DH)

        def one_block(accum, block_data):
            key_acc, value_acc = accum
            query_rows, grad_rows, ref_rows, live_rows = block_data
            query_wide = query_rows.astype(jnp.float32)
            grad_wide = grad_rows.astype(jnp.float32)
            key_sel = key_head[ref_rows].astype(jnp.float32)
            value_sel = value_head[ref_rows].astype(jnp.float32)
            scores = jnp.einsum("td,trcd->trc", query_wide, key_sel)
            scores = jnp.where(live_rows[:, :, None], scores, NEGATIVE)
            row_max = jnp.max(scores, axis=(1, 2), keepdims=True)
            log_total = row_max + jnp.log(jnp.sum(jnp.exp(scores - row_max), axis=(1, 2), keepdims=True))
            soft_weights = jnp.exp(scores - log_total)
            rounded_wide = lax.optimization_barrier(soft_weights.astype(jnp.bfloat16)).astype(jnp.float32)
            attended = jnp.einsum("trc,trcd->td", rounded_wide, value_sel)
            row_term = jnp.sum(grad_wide * attended, axis=1)
            weight_grad = jnp.einsum("td,trcd->trc", grad_wide, value_sel)
            score_grad = (soft_weights * (weight_grad - row_term[:, None, None])).astype(jnp.bfloat16)
            score_wide = lax.optimization_barrier(score_grad).astype(jnp.float32)
            query_term = jnp.einsum("trc,trcd->td", score_wide, key_sel)
            key_terms = jnp.einsum("trc,td->trcd", score_wide, query_wide)
            value_terms = jnp.einsum("trc,td->trcd", rounded_wide, grad_wide)
            key_acc = key_acc.at[ref_rows].add(key_terms)
            value_acc = value_acc.at[ref_rows].add(value_terms)
            return (key_acc, value_acc), (attended, query_term)

        zero_grid = jnp.zeros((block_count, BLOCK, DH), jnp.float32)
        sums, rows_out = lax.scan(one_block, (zero_grid, zero_grid), (query_split, grad_split, refs_split, live_split))
        attended, query_term = rows_out
        key_acc, value_acc = sums
        return carry, (attended.reshape(token_count, DH), query_term.reshape(token_count, DH),
                       key_acc.reshape(cell_count, DH), value_acc.reshape(cell_count, DH))

    unused, outputs = lax.scan(one_head, jnp.zeros((), jnp.float32), (head_queries, head_grads, head_keys, head_values))
    attended, query_term, key_term, value_term = outputs
    context = attended.transpose(1, 0, 2).reshape(token_count, HEADS * DH).astype(jnp.bfloat16)
    query_grad = query_term.transpose(1, 0, 2).reshape(token_count, HEADS * DH).astype(jnp.bfloat16)
    key_grad = key_term.transpose(1, 0, 2).reshape(cell_count, HEADS * DH).astype(jnp.bfloat16)
    value_grad = value_term.transpose(1, 0, 2).reshape(cell_count, HEADS * DH).astype(jnp.bfloat16)
    return (context, query_grad, key_grad, value_grad)
```

```python
import functools

import jax
import jax.numpy as jnp
import numpy as np
from jax import lax
from jax.experimental import pallas as pl
from jax.experimental.pallas import tpu as pltpu
from jax.sharding import PartitionSpec as P

DH = 64
BLOCK = 128
HIDDEN = -1e30
LANES = 128


def nt(a, b):
    return lax.dot_general(a, b, (((1,), (1,)), ((), ())), preferred_element_type=jnp.float32)


def nn(a, b):
    return lax.dot_general(a, b, (((1,), (0,)), ((), ())), preferred_element_type=jnp.float32)


def attention_kernel(
    heads, chunk, k_ref, v_ref, e_ref, q_ref, g_ref, bias_ref,
    ctx_ref, dq_ref, dk_ref, dv_ref,
    kt, vt, s_buf, e_buf, dk_acc, dv_acc,
):
    step = pl.program_id(0)
    cells, width = k_ref.shape
    rows = q_ref.shape[0]
    chunks = cells // chunk

    @pl.when(step == 0)
    def _():
        def prepare(i, _):
            at = pl.ds(pl.multiple_of(i * chunk, chunk), chunk)
            kt[:, at] = k_ref[at, :].T
            vt[:, at] = v_ref[at, :].T
            dk_acc[at, :] = jnp.zeros((chunk, width), jnp.float32)
            dv_acc[at, :] = jnp.zeros((chunk, width), jnp.float32)
            return 0

        lax.fori_loop(0, chunks, prepare, 0)

    lane = lax.broadcasted_iota(jnp.int32, (rows, width), 1)
    own = [(lane >= h * DH) & (lane < (h + 1) * DH) for h in range(heads)]
    q = q_ref[...]
    q_own = [jnp.where(own[h], q, jnp.zeros_like(q)) for h in range(heads)]
    q_aug = [jnp.concatenate([q_own[h], bias_ref[...]], axis=1) for h in range(heads)]

    def score_chunk(i, tops):
        at = pl.ds(pl.multiple_of(i * chunk, chunk), chunk)
        left = jnp.concatenate([k_ref[at, :], e_ref[at, :]], axis=1)
        out = []
        for h in range(heads):
            s = nt(left, q_aug[h])
            s_buf[h, at, :] = s
            out.append(jnp.maximum(tops[h], jnp.max(s.reshape(chunk // 8, 8, rows), axis=0)))
        return tuple(out)

    tops = lax.fori_loop(
        0, chunks, score_chunk, tuple(jnp.full((8, rows), -3e38, jnp.float32) for _ in range(heads))
    )
    top = [jnp.max(t, axis=0, keepdims=True) for t in tops]

    def weight_chunk(i, carry):
        at = pl.ds(pl.multiple_of(i * chunk, chunk), chunk)
        totals, outs = carry
        new_totals, new_outs = [], []
        for h in range(heads):
            e = jnp.exp(s_buf[h, at, :] - top[h])
            new_totals.append(totals[h] + jnp.sum(e.reshape(chunk // 8, 8, rows), axis=0))
            e = e.astype(jnp.bfloat16)
            e_buf[h, at, :] = e
            new_outs.append(outs[h] + nn(vt[h * DH : (h + 1) * DH, at], e))
        return tuple(new_totals), tuple(new_outs)

    totals, outs = lax.fori_loop(
        0,
        chunks,
        weight_chunk,
        (
            tuple(jnp.zeros((8, rows), jnp.float32) for _ in range(heads)),
            tuple(jnp.zeros((DH, rows), jnp.float32) for _ in range(heads)),
        ),
    )
    inv = [1.0 / jnp.sum(t, axis=0, keepdims=True) for t in totals]
    stack = jnp.concatenate(
        [outs[h] * inv[h] for h in range(heads)]
        + [jnp.broadcast_to(inv[h], (DH, rows)) for h in range(heads)],
        axis=0,
    ).T
    attended = stack[:, :width]
    ctx_ref[...] = attended.astype(ctx_ref.dtype)
    g_scaled = (g_ref[...].astype(jnp.float32) * stack[:, width:]).astype(jnp.bfloat16)
    product = g_scaled.astype(jnp.float32) * attended
    lane_aug = lax.broadcasted_iota(jnp.int32, (rows, LANES), 1)
    g_own, g_aug = [], []
    for h in range(heads):
        term = -jnp.sum(jnp.where(own[h], product, 0.0), axis=1, keepdims=True)
        high = term.astype(jnp.bfloat16).astype(jnp.float32)
        low = term - high
        extra = jnp.where(
            lane_aug == LANES - 1, high, jnp.where(lane_aug == LANES - 2, low, 0.0)
        ).astype(jnp.bfloat16)
        g_own.append(jnp.where(own[h], g_scaled, jnp.zeros_like(g_scaled)))
        g_aug.append(jnp.concatenate([g_own[h], extra], axis=1))
    q_all = jnp.concatenate(q_own, axis=0)
    g_all = jnp.concatenate(g_own, axis=0)

    def grad_chunk(i, dqs):
        at = pl.ds(pl.multiple_of(i * chunk, chunk), chunk)
        left = jnp.concatenate([v_ref[at, :], e_ref[at, :]], axis=1)
        new_dqs, ds_all, e_all = [], [], []
        for h in range(heads):
            e = e_buf[h, at, :]
            ds = (e.astype(jnp.float32) * nt(left, g_aug[h])).astype(jnp.bfloat16)
            new_dqs.append(dqs[h] + nn(kt[h * DH : (h + 1) * DH, at], ds))
            ds_all.append(ds)
            e_all.append(e)
        dk_acc[at, :] += nn(jnp.concatenate(ds_all, axis=1), q_all)
        dv_acc[at, :] += nn(jnp.concatenate(e_all, axis=1), g_all)
        return tuple(new_dqs)

    dqs = lax.fori_loop(
        0, chunks, grad_chunk, tuple(jnp.zeros((DH, rows), jnp.float32) for _ in range(heads))
    )
    dq_ref[...] = jnp.concatenate(dqs, axis=0).T.astype(dq_ref.dtype)

    @pl.when(step == pl.num_programs(0) - 1)
    def _():
        dk_ref[...] = dk_acc[...].astype(dk_ref.dtype)
        dv_ref[...] = dv_acc[...].astype(dv_ref.dtype)


def cell_marks(cells):
    block_ids = lax.broadcasted_iota(jnp.int32, (cells, LANES), 0) // BLOCK
    lane = lax.broadcasted_iota(jnp.int32, (cells, LANES), 1)
    return ((block_ids == lane) | (lane >= LANES - 2)).astype(jnp.bfloat16)


def attention(q, g, k, v, bias, grad_type=jnp.bfloat16, rows=256, chunk=512):
    tokens, width = q.shape
    cells = k.shape[0]
    heads = width // DH
    whole = lambda i: (0, 0)
    part = lambda i: (i, 0)
    cell_spec = pl.BlockSpec((cells, width), whole)
    token_spec = pl.BlockSpec((rows, width), part)
    bf = jnp.bfloat16
    return pl.pallas_call(
        functools.partial(attention_kernel, heads, chunk),
        grid=(tokens // rows,),
        out_shape=(
            jax.ShapeDtypeStruct((tokens, width), bf),
            jax.ShapeDtypeStruct((tokens, width), bf),
            jax.ShapeDtypeStruct((cells, width), grad_type),
            jax.ShapeDtypeStruct((cells, width), grad_type),
        ),
        in_specs=[
            cell_spec,
            cell_spec,
            pl.BlockSpec((cells, LANES), whole),
            token_spec,
            token_spec,
            pl.BlockSpec((rows, LANES), part),
        ],
        out_specs=(token_spec, token_spec, cell_spec, cell_spec),
        scratch_shapes=[
            pltpu.VMEM((width, cells), bf),
            pltpu.VMEM((width, cells), bf),
            pltpu.VMEM((heads, cells, rows), jnp.float32),
            pltpu.VMEM((heads, cells, rows), bf),
            pltpu.VMEM((cells, width), jnp.float32),
            pltpu.VMEM((cells, width), jnp.float32),
        ],
        compiler_params=pltpu.CompilerParams(vmem_limit_bytes=60 * 1024 * 1024),
        name="attention",
    )(k, v, cell_marks(cells), q, g, bias)


def hidden_blocks(ref_blocks, ref_counts):
    slot_ids = jnp.arange(ref_blocks.shape[1], dtype=jnp.int32)
    live = slot_ids[None, :] < ref_counts[:, None]
    lane = jnp.arange(LANES, dtype=jnp.int32)
    seen = jnp.any((ref_blocks[:, :, None] == lane) & live[:, :, None], axis=1)
    return jnp.where(seen | (lane >= LANES - 2), 0.0, HIDDEN).astype(jnp.bfloat16)


def shared_head(q, g, k, v, bias, per, dec):
    share = DH // q.shape[1]
    mates = [
        [per * (j + i) + c for i in range(share)] for c in range(per) for j in range(0, dec, share)
    ]
    place = lax.rem(lax.axis_index("enc") // per, share)
    rows = q.shape[0] // share

    def to_head(x):
        return lax.all_to_all(x, "enc", 0, 1, axis_index_groups=mates, tiled=True)

    def from_head(x):
        return lax.all_to_all(x, "enc", 1, 0, axis_index_groups=mates, tiled=True)

    def widen(x):
        return lax.all_gather(x, "enc", axis=1, axis_index_groups=mates, tiled=True)

    def add_up(x):
        total = lax.psum_scatter(
            x, "enc", scatter_dimension=1, axis_index_groups=mates, tiled=True
        )
        return total.astype(jnp.bfloat16)

    bias = lax.dynamic_slice_in_dim(bias, place * rows, rows, 0)
    ctx, dq, dk, dv = attention(to_head(q), to_head(g), widen(k), widen(v), bias, jnp.float32)
    return from_head(ctx), from_head(dq), add_up(dk), add_up(dv)


def body(queries, out_grad, memory_keys, memory_values, ref_blocks, ref_counts):
    enc, dec = lax.axis_size("enc"), lax.axis_size("dec")
    per = enc // dec
    tok, tok_width = queries.shape
    own_cells, full = memory_keys.shape
    width = full // (enc * dec)
    groups = [[per * k + c for k in range(dec)] for c in range(per)]

    def token_in(x):
        x = x.reshape(tok, dec, width).transpose(1, 0, 2)
        x = lax.all_to_all(x, "enc", 0, 0, axis_index_groups=groups)
        return lax.all_to_all(x, "dec", 0, 0).reshape(dec * tok, width)

    def token_out(x):
        x = lax.all_to_all(x.reshape(dec, tok, width), "dec", 0, 0)
        x = lax.all_to_all(x, "enc", 0, 0, axis_index_groups=groups)
        return x.transpose(1, 0, 2).reshape(tok, tok_width)

    def cell_in(x):
        x = lax.dynamic_slice_in_dim(x, lax.axis_index("dec") * (full // dec), full // dec, 1)
        x = x.reshape(own_cells, per, dec, width).transpose(2, 1, 0, 3)
        x = lax.all_to_all(x.reshape(enc, own_cells, width), "enc", 0, 0)
        return x.reshape(enc * own_cells, width)

    def cell_out(x):
        x = lax.all_to_all(x.reshape(enc, own_cells, width), "enc", 0, 0)
        x = x.reshape(dec, per, own_cells, width).transpose(2, 1, 0, 3)
        return x.reshape(own_cells, full // dec)

    bias = lax.all_gather(hidden_blocks(ref_blocks, ref_counts), "dec", tiled=True)
    q, g, k, v = token_in(queries), token_in(out_grad), cell_in(memory_keys), cell_in(memory_values)
    if width >= DH:
        ctx, dq, dk, dv = attention(q, g, k, v, bias)
    else:
        ctx, dq, dk, dv = shared_head(q, g, k, v, bias, per, dec)
    return token_out(ctx), token_out(dq), cell_out(dk), cell_out(dv)


def solution(mesh):
    in_specs = (
        P("dec", "enc"),
        P("dec", "enc"),
        P("enc", None),
        P("enc", None),
        P("dec", None),
        P("dec"),
    )
    out_specs = (P("dec", "enc"), P("dec", "enc"), P("enc", "dec"), P("enc", "dec"))
    return jax.shard_map(body, mesh=mesh, in_specs=in_specs, out_specs=out_specs, check_vma=False)
```

```python
import functools

import jax
import jax.numpy as jnp
import numpy as np
from jax import lax
from jax.experimental import pallas as pl
from jax.experimental.pallas import tpu as pltpu
from jax.sharding import PartitionSpec as P

DH = 64
BLOCK = 128
HIDDEN = -1e30
LANES = 128


def nt(a, b):
    return lax.dot_general(a, b, (((1,), (1,)), ((), ())), preferred_element_type=jnp.float32)


def nn(a, b):
    return lax.dot_general(a, b, (((1,), (0,)), ((), ())), preferred_element_type=jnp.float32)


def attention_kernel(
    heads, chunk, k_ref, v_ref, e_ref, q_ref, g_ref, bias_ref,
    ctx_ref, dq_ref, dk_ref, dv_ref,
    kt, vt, s_buf, e_buf, dk_acc, dv_acc,
):
    step = pl.program_id(0)
    cells, width = k_ref.shape
    rows = q_ref.shape[0]
    chunks = cells // chunk

    @pl.when(step == 0)
    def _():
        def prepare(i, _):
            at = pl.ds(pl.multiple_of(i * chunk, chunk), chunk)
            kt[:, at] = k_ref[at, :].T
            vt[:, at] = v_ref[at, :].T
            dk_acc[at, :] = jnp.zeros((chunk, width), jnp.float32)
            dv_acc[at, :] = jnp.zeros((chunk, width), jnp.float32)
            return 0

        lax.fori_loop(0, chunks, prepare, 0)

    lane = lax.broadcasted_iota(jnp.int32, (rows, width), 1)
    own = [(lane >= h * DH) & (lane < (h + 1) * DH) for h in range(heads)]
    q = q_ref[...]
    q_own = [jnp.where(own[h], q, jnp.zeros_like(q)) for h in range(heads)]
    bias = bias_ref[...].astype(jnp.float32)
    blank = jnp.zeros((LANES - bias.shape[0], rows), jnp.float32)
    bias = jnp.concatenate([bias, blank], axis=0).T.astype(jnp.bfloat16)
    q_aug = [jnp.concatenate([q_own[h], bias], axis=1) for h in range(heads)]

    def score_chunk(i, tops):
        at = pl.ds(pl.multiple_of(i * chunk, chunk), chunk)
        left = jnp.concatenate([k_ref[at, :], e_ref[at, :]], axis=1)
        out = []
        for h in range(heads):
            s = nt(left, q_aug[h])
            s_buf[h, at, :] = s
            out.append(jnp.maximum(tops[h], jnp.max(s.reshape(chunk // 8, 8, rows), axis=0)))
        return tuple(out)

    tops = lax.fori_loop(
        0, chunks, score_chunk, tuple(jnp.full((8, rows), -3e38, jnp.float32) for _ in range(heads))
    )
    top = [jnp.max(t, axis=0, keepdims=True) for t in tops]

    def weight_chunk(i, carry):
        at = pl.ds(pl.multiple_of(i * chunk, chunk), chunk)
        totals, outs = carry
        new_totals, new_outs = [], []
        for h in range(heads):
            e = jnp.exp(s_buf[h, at, :] - top[h])
            new_totals.append(totals[h] + jnp.sum(e.reshape(chunk // 8, 8, rows), axis=0))
            e = e.astype(jnp.bfloat16)
            e_buf[h, at, :] = e
            new_outs.append(outs[h] + nn(vt[h * DH : (h + 1) * DH, at], e))
        return tuple(new_totals), tuple(new_outs)

    totals, outs = lax.fori_loop(
        0,
        chunks,
        weight_chunk,
        (
            tuple(jnp.zeros((8, rows), jnp.float32) for _ in range(heads)),
            tuple(jnp.zeros((DH, rows), jnp.float32) for _ in range(heads)),
        ),
    )
    inv = [1.0 / jnp.sum(t, axis=0, keepdims=True) for t in totals]
    stack = jnp.concatenate(
        [outs[h] * inv[h] for h in range(heads)]
        + [jnp.broadcast_to(inv[h], (DH, rows)) for h in range(heads)],
        axis=0,
    ).T
    attended = stack[:, :width]
    ctx_ref[...] = attended.astype(ctx_ref.dtype)
    g_scaled = (g_ref[...].astype(jnp.float32) * stack[:, width:]).astype(jnp.bfloat16)
    product = g_scaled.astype(jnp.float32) * attended
    lane_aug = lax.broadcasted_iota(jnp.int32, (rows, LANES), 1)
    g_own, g_aug = [], []
    for h in range(heads):
        term = -jnp.sum(jnp.where(own[h], product, 0.0), axis=1, keepdims=True)
        high = term.astype(jnp.bfloat16).astype(jnp.float32)
        low = term - high
        extra = jnp.where(
            lane_aug == LANES - 1, high, jnp.where(lane_aug == LANES - 2, low, 0.0)
        ).astype(jnp.bfloat16)
        g_own.append(jnp.where(own[h], g_scaled, jnp.zeros_like(g_scaled)))
        g_aug.append(jnp.concatenate([g_own[h], extra], axis=1))
    q_all = jnp.concatenate(q_own, axis=0)
    g_all = jnp.concatenate(g_own, axis=0)

    def grad_chunk(i, dqs):
        at = pl.ds(pl.multiple_of(i * chunk, chunk), chunk)
        left = jnp.concatenate([v_ref[at, :], e_ref[at, :]], axis=1)
        new_dqs, ds_all, e_all = [], [], []
        for h in range(heads):
            e = e_buf[h, at, :]
            ds = (e.astype(jnp.float32) * nt(left, g_aug[h])).astype(jnp.bfloat16)
            new_dqs.append(dqs[h] + nn(kt[h * DH : (h + 1) * DH, at], ds))
            ds_all.append(ds)
            e_all.append(e)
        dk_acc[at, :] += nn(jnp.concatenate(ds_all, axis=1), q_all)
        dv_acc[at, :] += nn(jnp.concatenate(e_all, axis=1), g_all)
        return tuple(new_dqs)

    dqs = lax.fori_loop(
        0, chunks, grad_chunk, tuple(jnp.zeros((DH, rows), jnp.float32) for _ in range(heads))
    )
    dq_ref[...] = jnp.concatenate(dqs, axis=0).T.astype(dq_ref.dtype)

    @pl.when(step == pl.num_programs(0) - 1)
    def _():
        dk_ref[...] = dk_acc[...].astype(dk_ref.dtype)
        dv_ref[...] = dv_acc[...].astype(dv_ref.dtype)


def cell_marks(cells):
    block_ids = lax.broadcasted_iota(jnp.int32, (cells, LANES), 0) // BLOCK
    lane = lax.broadcasted_iota(jnp.int32, (cells, LANES), 1)
    return ((block_ids == lane) | (lane >= LANES - 2)).astype(jnp.bfloat16)


def attention(q, g, k, v, bias, grad_type=jnp.bfloat16, rows=256, chunk=512):
    tokens, width = q.shape
    cells = k.shape[0]
    heads = width // DH
    whole = lambda i: (0, 0)
    part = lambda i: (i, 0)
    cell_spec = pl.BlockSpec((cells, width), whole)
    token_spec = pl.BlockSpec((rows, width), part)
    bf = jnp.bfloat16
    return pl.pallas_call(
        functools.partial(attention_kernel, heads, chunk),
        grid=(tokens // rows,),
        out_shape=(
            jax.ShapeDtypeStruct((tokens, width), bf),
            jax.ShapeDtypeStruct((tokens, width), bf),
            jax.ShapeDtypeStruct((cells, width), grad_type),
            jax.ShapeDtypeStruct((cells, width), grad_type),
        ),
        in_specs=[
            cell_spec,
            cell_spec,
            pl.BlockSpec((cells, LANES), whole),
            token_spec,
            token_spec,
            pl.BlockSpec((bias.shape[0], rows), lambda i: (0, i)),
        ],
        out_specs=(token_spec, token_spec, cell_spec, cell_spec),
        scratch_shapes=[
            pltpu.VMEM((width, cells), bf),
            pltpu.VMEM((width, cells), bf),
            pltpu.VMEM((heads, cells, rows), jnp.float32),
            pltpu.VMEM((heads, cells, rows), bf),
            pltpu.VMEM((cells, width), jnp.float32),
            pltpu.VMEM((cells, width), jnp.float32),
        ],
        compiler_params=pltpu.CompilerParams(vmem_limit_bytes=60 * 1024 * 1024),
        name="attention",
    )(k, v, cell_marks(cells), q, g, bias)


def hidden_blocks(ref_blocks, ref_counts, blocks):
    slot_ids = jnp.arange(ref_blocks.shape[1], dtype=jnp.int32)
    live = slot_ids[None, :] < ref_counts[:, None]
    wanted = jnp.where(live, ref_blocks, -1).T
    seen = jnp.any(wanted[:, None, :] == jnp.arange(blocks, dtype=jnp.int32)[:, None], axis=0)
    return jnp.where(seen, 0.0, HIDDEN).astype(jnp.bfloat16)


def greet_all():
    barrier = pltpu.get_barrier_semaphore()
    enc, dec = lax.axis_size("enc"), lax.axis_size("dec")
    me = lax.axis_index("enc") * dec + lax.axis_index("dec")

    def greet(d, _):
        other = lax.rem(me + d, enc * dec)
        pl.semaphore_signal(
            barrier, inc=1, device_id=(other // dec, lax.rem(other, dec)),
            device_id_type=pl.DeviceIdType.MESH,
        )
        return 0

    lax.fori_loop(1, enc * dec, greet, 0)
    pl.semaphore_wait(barrier, enc * dec - 1)


def remote(src, dst, send, recv, target):
    return pltpu.make_async_remote_copy(
        src_ref=src, dst_ref=dst, send_sem=send, recv_sem=recv,
        device_id=target, device_id_type=pl.DeviceIdType.MESH,
    )


def lanes(ref, index, width):
    return ref.at[:, pl.ds(pl.multiple_of(index * width, width), width)]


def rows_of(ref, index, count):
    return ref.at[pl.ds(pl.multiple_of(index * count, count), count), :]


def scatter_kernel(
    q, k, bias, g, v, q_all, k_all, bias_all, g_all, v_all,
    tok_send, tok_recv, cell_send, cell_recv, bias_send, bias_recv, local,
):
    enc, dec = lax.axis_size("enc"), lax.axis_size("dec")
    per = enc // dec
    e, z = lax.axis_index("enc"), lax.axis_index("dec")
    width = k_all.shape[1]
    tok, cells = q.shape[0], k.shape[0]
    home, core = e // per, lax.rem(e, per)
    slot = lambda x: z * enc + lax.rem(x, per) * dec + x // per
    greet_all()

    def token_copy(n, src, dst, i):
        return remote(
            lanes(src, i, width), rows_of(dst, z, tok),
            tok_send.at[n, i], tok_recv.at[n, z], (per * i + core, home),
        )

    def token_wait(n, src, dst, i):
        return remote(
            lanes(src, 0, width), rows_of(dst, i, tok),
            tok_send.at[n, 0], tok_recv.at[n, i], (e, z),
        )

    def token_own(n, src, dst):
        return pltpu.make_async_copy(lanes(src, home, width), rows_of(dst, z, tok), local.at[n])

    def cell_copy(n, src, dst, j):
        target = lax.rem(e + j, enc)
        return remote(
            lanes(src, slot(target), width), rows_of(dst, e, cells),
            cell_send.at[n, j - 1], cell_recv.at[n, j - 1], (target, z),
        )

    def cell_wait(n, src, dst, j):
        origin = lax.rem(e - j + enc, enc)
        return remote(
            lanes(src, 0, width), rows_of(dst, origin, cells),
            cell_send.at[n, j - 1], cell_recv.at[n, j - 1], (origin, z),
        )

    def cell_own(n, src, dst):
        return pltpu.make_async_copy(
            lanes(src, slot(e), width), rows_of(dst, e, cells), local.at[2 + n]
        )

    def bias_copy(j):
        target = lax.rem(z + j, dec)
        return remote(
            bias, lanes(bias_all, z, tok), bias_send.at[j - 1], bias_recv.at[j - 1], (e, target)
        )

    def bias_wait(j):
        origin = lax.rem(z - j + dec, dec)
        return remote(
            bias, lanes(bias_all, origin, tok), bias_send.at[j - 1], bias_recv.at[j - 1], (e, origin)
        )

    bias_own = pltpu.make_async_copy(bias, lanes(bias_all, z, tok), local.at[4])
    staged = ((0, q, q_all, k, k_all), (1, g, g_all, v, v_all))
    for n, ts, td, cs, cd in staged:
        for i in range(dec):
            mine = (home == z) & (z == i)
            pl.when(jnp.logical_not(mine))(lambda: token_copy(n, ts, td, i).start())
        pl.when(home == z)(lambda: token_own(n, ts, td).start())
        if n == 0:
            for j in range(1, dec):
                bias_copy(j).start()
            bias_own.start()
        for j in range(1, enc):
            cell_copy(n, cs, cd, j).start()
        cell_own(n, cs, cd).start()
    for n, ts, td, cs, cd in staged:
        for i in range(dec):
            mine = (home == z) & (z == i)
            pl.when(jnp.logical_not(mine))(lambda: token_copy(n, ts, td, i).wait_send())
            pl.when(jnp.logical_not(mine))(lambda: token_wait(n, ts, td, i).wait_recv())
        pl.when(home == z)(lambda: token_own(n, ts, td).wait())
        for j in range(1, enc):
            cell_copy(n, cs, cd, j).wait_send()
            cell_wait(n, cs, cd, j).wait_recv()
        cell_own(n, cs, cd).wait()
    for j in range(1, dec):
        bias_copy(j).wait_send()
        bias_wait(j).wait_recv()
    bias_own.wait()


def gather_kernel(
    *refs
):
    enc, dec = lax.axis_size("enc"), lax.axis_size("dec")
    per = enc // dec
    e, z = lax.axis_index("enc"), lax.axis_index("dec")
    t0, t1, c0, c1, o0, o1, d0, d1, tok_send, tok_recv, cell_send, cell_recv, local = refs
    width = t0.shape[1]
    tok, cells = o0.shape[0], d0.shape[0]
    home, core = e // per, lax.rem(e, per)
    slot = lambda x: lax.rem(x, per) * dec + x // per
    greet_all()

    def token_copy(n, src, dst, i):
        return remote(
            rows_of(src, i, tok), lanes(dst, home, width),
            tok_send.at[n, i], tok_recv.at[n, home], (per * z + core, i),
        )

    def token_wait(n, src, dst, i):
        return remote(
            rows_of(src, 0, tok), lanes(dst, i, width),
            tok_send.at[n, 0], tok_recv.at[n, i], (e, z),
        )

    def token_own(n, src, dst):
        return pltpu.make_async_copy(rows_of(src, z, tok), lanes(dst, home, width), local.at[n])

    def cell_copy(n, src, dst, j):
        target = lax.rem(e + j, enc)
        return remote(
            rows_of(src, target, cells), lanes(dst, slot(e), width),
            cell_send.at[n, j - 1], cell_recv.at[n, j - 1], (target, z),
        )

    def cell_wait(n, src, dst, j):
        origin = lax.rem(e - j + enc, enc)
        return remote(
            rows_of(src, 0, cells), lanes(dst, slot(origin), width),
            cell_send.at[n, j - 1], cell_recv.at[n, j - 1], (origin, z),
        )

    def cell_own(n, src, dst):
        return pltpu.make_async_copy(
            rows_of(src, e, cells), lanes(dst, slot(e), width), local.at[2 + n]
        )

    staged = ((0, t0, o0, c0, d0), (1, t1, o1, c1, d1))
    for n, ts, td, cs, cd in staged:
        for i in range(dec):
            mine = (home == z) & (z == i)
            pl.when(jnp.logical_not(mine))(lambda: token_copy(n, ts, td, i).start())
        pl.when(home == z)(lambda: token_own(n, ts, td).start())
        for j in range(1, enc):
            cell_copy(n, cs, cd, j).start()
        cell_own(n, cs, cd).start()
    for n, ts, td, cs, cd in staged:
        for i in range(dec):
            mine = (home == z) & (z == i)
            pl.when(jnp.logical_not(mine))(lambda: token_copy(n, ts, td, i).wait_send())
            pl.when(jnp.logical_not(mine))(lambda: token_wait(n, ts, td, i).wait_recv())
        pl.when(home == z)(lambda: token_own(n, ts, td).wait())
        for j in range(1, enc):
            cell_copy(n, cs, cd, j).wait_send()
            cell_wait(n, cs, cd, j).wait_recv()
        cell_own(n, cs, cd).wait()


def scatter(q, k, bias, g, v):
    enc, dec = lax.axis_size("enc"), lax.axis_size("dec")
    width = k.shape[1] // (enc * dec)
    bf = jnp.bfloat16
    dma = pltpu.SemaphoreType.DMA
    tokens = jax.ShapeDtypeStruct((dec * q.shape[0], width), bf)
    cells = jax.ShapeDtypeStruct((enc * k.shape[0], width), bf)
    return pl.pallas_call(
        scatter_kernel,
        out_shape=(
            tokens, cells, jax.ShapeDtypeStruct((bias.shape[0], dec * bias.shape[1]), bf), tokens, cells
        ),
        in_specs=[pl.BlockSpec(memory_space=pl.ANY)] * 5,
        out_specs=[pl.BlockSpec(memory_space=pl.ANY)] * 5,
        scratch_shapes=[
            dma((2, dec)), dma((2, dec)), dma((2, enc - 1)), dma((2, enc - 1)),
            dma((dec - 1,)), dma((dec - 1,)), dma((5,)),
        ],
        compiler_params=pltpu.CompilerParams(collective_id=0, has_side_effects=True),
        name="scatter_in",
    )(q, k, bias, g, v)


def gather(ctx, dq, dk, dv, tok, cells):
    enc, dec = lax.axis_size("enc"), lax.axis_size("dec")
    width = ctx.shape[1]
    bf = jnp.bfloat16
    dma = pltpu.SemaphoreType.DMA
    token_out = jax.ShapeDtypeStruct((tok, dec * width), bf)
    cell_out = jax.ShapeDtypeStruct((cells, enc * width), bf)
    return pl.pallas_call(
        gather_kernel,
        out_shape=(token_out, token_out, cell_out, cell_out),
        in_specs=[pl.BlockSpec(memory_space=pl.ANY)] * 4,
        out_specs=[pl.BlockSpec(memory_space=pl.ANY)] * 4,
        scratch_shapes=[
            dma((2, dec)), dma((2, dec)), dma((2, enc - 1)), dma((2, enc - 1)), dma((4,)),
        ],
        compiler_params=pltpu.CompilerParams(collective_id=1, has_side_effects=True),
        name="gather_out",
    )(ctx, dq, dk, dv)


def shared_head(q, g, k, v, bias, per, dec):
    share = DH // q.shape[1]
    mates = [
        [per * (j + i) + c for i in range(share)] for c in range(per) for j in range(0, dec, share)
    ]
    place = lax.rem(lax.axis_index("enc") // per, share)
    rows = q.shape[0] // share

    def to_head(x):
        return lax.all_to_all(x, "enc", 0, 1, axis_index_groups=mates, tiled=True)

    def from_head(x):
        return lax.all_to_all(x, "enc", 1, 0, axis_index_groups=mates, tiled=True)

    def widen(x):
        return lax.all_gather(x, "enc", axis=1, axis_index_groups=mates, tiled=True)

    def add_up(x):
        total = lax.psum_scatter(
            x, "enc", scatter_dimension=1, axis_index_groups=mates, tiled=True
        )
        return total.astype(jnp.bfloat16)

    bias = lax.dynamic_slice_in_dim(bias, place * rows, rows, 1)
    ctx, dq, dk, dv = attention(to_head(q), to_head(g), widen(k), widen(v), bias, jnp.float32)
    return from_head(ctx), from_head(dq), add_up(dk), add_up(dv)


def body(queries, out_grad, memory_keys, memory_values, ref_blocks, ref_counts):
    enc, dec = lax.axis_size("enc"), lax.axis_size("dec")
    per = enc // dec
    tok, tok_width = queries.shape
    own_cells, full = memory_keys.shape
    width = full // (enc * dec)
    groups = [[per * k + c for k in range(dec)] for c in range(per)]

    def token_in(x):
        x = x.reshape(tok, dec, width).transpose(1, 0, 2)
        x = lax.all_to_all(x, "enc", 0, 0, axis_index_groups=groups)
        return lax.all_to_all(x, "dec", 0, 0).reshape(dec * tok, width)

    def token_out(x):
        x = lax.all_to_all(x.reshape(dec, tok, width), "dec", 0, 0)
        x = lax.all_to_all(x, "enc", 0, 0, axis_index_groups=groups)
        return x.transpose(1, 0, 2).reshape(tok, tok_width)

    def cell_in(x):
        x = lax.dynamic_slice_in_dim(x, lax.axis_index("dec") * (full // dec), full // dec, 1)
        x = x.reshape(own_cells, per, dec, width).transpose(2, 1, 0, 3)
        x = lax.all_to_all(x.reshape(enc, own_cells, width), "enc", 0, 0)
        return x.reshape(enc * own_cells, width)

    def cell_out(x):
        x = lax.all_to_all(x.reshape(enc, own_cells, width), "enc", 0, 0)
        x = x.reshape(dec, per, own_cells, width).transpose(2, 1, 0, 3)
        return x.reshape(own_cells, full // dec)

    bias = hidden_blocks(ref_blocks, ref_counts, enc * own_cells // BLOCK)
    if width % LANES == 0:
        q, k, bias, g, v = scatter(queries, memory_keys, bias, out_grad, memory_values)
        return gather(*attention(q, g, k, v, bias), tok, own_cells)
    bias = lax.all_gather(bias, "dec", axis=1, tiled=True)
    q, g, k, v = token_in(queries), token_in(out_grad), cell_in(memory_keys), cell_in(memory_values)
    if width >= DH:
        ctx, dq, dk, dv = attention(q, g, k, v, bias)
    else:
        ctx, dq, dk, dv = shared_head(q, g, k, v, bias, per, dec)
    return token_out(ctx), token_out(dq), cell_out(dk), cell_out(dv)


def solution(mesh):
    in_specs = (
        P("dec", "enc"),
        P("dec", "enc"),
        P("enc", None),
        P("enc", None),
        P("dec", None),
        P("dec"),
    )
    out_specs = (P("dec", "enc"), P("dec", "enc"), P("enc", "dec"), P("enc", "dec"))
    return jax.shard_map(body, mesh=mesh, in_specs=in_specs, out_specs=out_specs, check_vma=False)
```

```python
import functools

import jax
import jax.numpy as jnp
import numpy as np
from jax import lax
from jax.experimental import pallas as pl
from jax.experimental.pallas import tpu as pltpu
from jax.sharding import PartitionSpec as P

DH = 64
BLOCK = 128
HIDDEN = -1e30
LANES = 128


def nt(a, b):
    return lax.dot_general(a, b, (((1,), (1,)), ((), ())), preferred_element_type=jnp.float32)


def nn(a, b):
    return lax.dot_general(a, b, (((1,), (0,)), ((), ())), preferred_element_type=jnp.float32)


def attention_kernel(
    heads, chunk, k_ref, v_ref, e_ref, q_ref, g_ref, bias_ref,
    ctx_ref, dq_ref, dk_ref, dv_ref,
    kt, vt, s_buf, e_buf, dk_acc, dv_acc,
):
    step = pl.program_id(0)
    cells, width = k_ref.shape
    rows = q_ref.shape[0]
    chunks = cells // chunk

    @pl.when(step == 0)
    def _():
        def prepare(i, _):
            at = pl.ds(pl.multiple_of(i * chunk, chunk), chunk)
            kt[:, at] = k_ref[at, :].T
            vt[:, at] = v_ref[at, :].T
            dk_acc[at, :] = jnp.zeros((chunk, width), jnp.float32)
            dv_acc[at, :] = jnp.zeros((chunk, width), jnp.float32)
            return 0

        lax.fori_loop(0, chunks, prepare, 0)

    lane = lax.broadcasted_iota(jnp.int32, (rows, width), 1)
    own = [(lane >= h * DH) & (lane < (h + 1) * DH) for h in range(heads)]
    q = q_ref[...]
    q_own = [jnp.where(own[h], q, jnp.zeros_like(q)) for h in range(heads)]
    bias = bias_ref[...].astype(jnp.float32)
    blank = jnp.zeros((LANES - bias.shape[0], rows), jnp.float32)
    bias = jnp.concatenate([bias, blank], axis=0).T.astype(jnp.bfloat16)
    q_aug = [jnp.concatenate([q_own[h], bias], axis=1) for h in range(heads)]

    def score_chunk(i, tops):
        at = pl.ds(pl.multiple_of(i * chunk, chunk), chunk)
        left = jnp.concatenate([k_ref[at, :], e_ref[at, :]], axis=1)
        out = []
        for h in range(heads):
            s = nt(left, q_aug[h])
            s_buf[h, at, :] = s
            out.append(jnp.maximum(tops[h], jnp.max(s.reshape(chunk // 8, 8, rows), axis=0)))
        return tuple(out)

    tops = lax.fori_loop(
        0, chunks, score_chunk, tuple(jnp.full((8, rows), -3e38, jnp.float32) for _ in range(heads))
    )
    top = [jnp.max(t, axis=0, keepdims=True) for t in tops]

    def weight_chunk(i, carry):
        at = pl.ds(pl.multiple_of(i * chunk, chunk), chunk)
        totals, outs = carry
        new_totals, new_outs = [], []
        for h in range(heads):
            e = jnp.exp(s_buf[h, at, :] - top[h])
            new_totals.append(totals[h] + jnp.sum(e.reshape(chunk // 8, 8, rows), axis=0))
            e = e.astype(jnp.bfloat16)
            e_buf[h, at, :] = e
            new_outs.append(outs[h] + nn(vt[h * DH : (h + 1) * DH, at], e))
        return tuple(new_totals), tuple(new_outs)

    totals, outs = lax.fori_loop(
        0,
        chunks,
        weight_chunk,
        (
            tuple(jnp.zeros((8, rows), jnp.float32) for _ in range(heads)),
            tuple(jnp.zeros((DH, rows), jnp.float32) for _ in range(heads)),
        ),
    )
    inv = [1.0 / jnp.sum(t, axis=0, keepdims=True) for t in totals]
    stack = jnp.concatenate(
        [outs[h] * inv[h] for h in range(heads)]
        + [jnp.broadcast_to(inv[h], (DH, rows)) for h in range(heads)],
        axis=0,
    ).T
    attended = stack[:, :width]
    ctx_ref[...] = attended.astype(ctx_ref.dtype)
    g_scaled = (g_ref[...].astype(jnp.float32) * stack[:, width:]).astype(jnp.bfloat16)
    product = g_scaled.astype(jnp.float32) * attended
    lane_aug = lax.broadcasted_iota(jnp.int32, (rows, LANES), 1)
    g_own, g_aug = [], []
    for h in range(heads):
        term = -jnp.sum(jnp.where(own[h], product, 0.0), axis=1, keepdims=True)
        high = term.astype(jnp.bfloat16).astype(jnp.float32)
        low = term - high
        extra = jnp.where(
            lane_aug == LANES - 1, high, jnp.where(lane_aug == LANES - 2, low, 0.0)
        ).astype(jnp.bfloat16)
        g_own.append(jnp.where(own[h], g_scaled, jnp.zeros_like(g_scaled)))
        g_aug.append(jnp.concatenate([g_own[h], extra], axis=1))
    q_all = jnp.concatenate(q_own, axis=0)
    g_all = jnp.concatenate(g_own, axis=0)

    def grad_chunk(i, dqs):
        at = pl.ds(pl.multiple_of(i * chunk, chunk), chunk)
        left = jnp.concatenate([v_ref[at, :], e_ref[at, :]], axis=1)
        new_dqs, ds_all, e_all = [], [], []
        for h in range(heads):
            e = e_buf[h, at, :]
            ds = (e.astype(jnp.float32) * nt(left, g_aug[h])).astype(jnp.bfloat16)
            new_dqs.append(dqs[h] + nn(kt[h * DH : (h + 1) * DH, at], ds))
            ds_all.append(ds)
            e_all.append(e)
        dk_acc[at, :] += nn(jnp.concatenate(ds_all, axis=1), q_all)
        dv_acc[at, :] += nn(jnp.concatenate(e_all, axis=1), g_all)
        return tuple(new_dqs)

    dqs = lax.fori_loop(
        0, chunks, grad_chunk, tuple(jnp.zeros((DH, rows), jnp.float32) for _ in range(heads))
    )
    dq_ref[...] = jnp.concatenate(dqs, axis=0).T.astype(dq_ref.dtype)

    @pl.when(step == pl.num_programs(0) - 1)
    def _():
        dk_ref[...] = dk_acc[...].astype(dk_ref.dtype)
        dv_ref[...] = dv_acc[...].astype(dv_ref.dtype)


def cell_marks(cells):
    block_ids = lax.broadcasted_iota(jnp.int32, (cells, LANES), 0) // BLOCK
    lane = lax.broadcasted_iota(jnp.int32, (cells, LANES), 1)
    return ((block_ids == lane) | (lane >= LANES - 2)).astype(jnp.bfloat16)


def attention(q, g, k, v, bias, grad_type=jnp.bfloat16, rows=512, chunk=2048):
    tokens, width = q.shape
    cells = k.shape[0]
    heads = width // DH
    chunk = min(chunk, cells)
    whole = lambda i: (0, 0)
    part = lambda i: (i, 0)
    cell_spec = pl.BlockSpec((cells, width), whole)
    token_spec = pl.BlockSpec((rows, width), part)
    bf = jnp.bfloat16
    return pl.pallas_call(
        functools.partial(attention_kernel, heads, chunk),
        grid=(tokens // rows,),
        out_shape=(
            jax.ShapeDtypeStruct((tokens, width), bf),
            jax.ShapeDtypeStruct((tokens, width), bf),
            jax.ShapeDtypeStruct((cells, width), grad_type),
            jax.ShapeDtypeStruct((cells, width), grad_type),
        ),
        in_specs=[
            cell_spec,
            cell_spec,
            pl.BlockSpec((cells, LANES), whole),
            token_spec,
            token_spec,
            pl.BlockSpec((bias.shape[0], rows), lambda i: (0, i)),
        ],
        out_specs=(token_spec, token_spec, cell_spec, cell_spec),
        scratch_shapes=[
            pltpu.VMEM((width, cells), bf),
            pltpu.VMEM((width, cells), bf),
            pltpu.VMEM((heads, cells, rows), jnp.float32),
            pltpu.VMEM((heads, cells, rows), bf),
            pltpu.VMEM((cells, width), jnp.float32),
            pltpu.VMEM((cells, width), jnp.float32),
        ],
        compiler_params=pltpu.CompilerParams(vmem_limit_bytes=60 * 1024 * 1024),
        name="attention",
    )(k, v, cell_marks(cells), q, g, bias)


def hidden_blocks(ref_blocks, ref_counts, blocks):
    slot_ids = jnp.arange(ref_blocks.shape[1], dtype=jnp.int32)
    live = slot_ids[None, :] < ref_counts[:, None]
    wanted = jnp.where(live, ref_blocks, -1).T
    seen = jnp.any(wanted[:, None, :] == jnp.arange(blocks, dtype=jnp.int32)[:, None], axis=0)
    return jnp.where(seen, 0.0, HIDDEN).astype(jnp.bfloat16)


def greet_all():
    barrier = pltpu.get_barrier_semaphore()
    enc, dec = lax.axis_size("enc"), lax.axis_size("dec")
    me = lax.axis_index("enc") * dec + lax.axis_index("dec")

    def greet(d, _):
        other = lax.rem(me + d, enc * dec)
        pl.semaphore_signal(
            barrier, inc=1, device_id=(other // dec, lax.rem(other, dec)),
            device_id_type=pl.DeviceIdType.MESH,
        )
        return 0

    lax.fori_loop(1, enc * dec, greet, 0)
    pl.semaphore_wait(barrier, enc * dec - 1)


def remote(src, dst, send, recv, target):
    return pltpu.make_async_remote_copy(
        src_ref=src, dst_ref=dst, send_sem=send, recv_sem=recv,
        device_id=target, device_id_type=pl.DeviceIdType.MESH,
    )


def lanes(ref, index, width):
    return ref.at[:, pl.ds(pl.multiple_of(index * width, width), width)]


def rows_of(ref, index, count):
    return ref.at[pl.ds(pl.multiple_of(index * count, count), count), :]


def scatter_kernel(
    q, k, bias, g, v, q_all, k_all, bias_all, g_all, v_all, q_mid, g_mid,
    mid_send, mid_recv, tok_send, tok_recv, cell_send, cell_recv, bias_send, bias_recv, local,
):
    enc, dec = lax.axis_size("enc"), lax.axis_size("dec")
    per = enc // dec
    e, z = lax.axis_index("enc"), lax.axis_index("dec")
    width = k_all.shape[1]
    tok, cells = q.shape[0], k.shape[0]
    home, core = e // per, lax.rem(e, per)
    slot = lambda x: z * enc + lax.rem(x, per) * dec + x // per
    around = lambda x, d: lax.rem(x + d + dec, dec)
    greet_all()

    def plane_copy(n, src, mid, d):
        i = around(home, d)
        return remote(
            lanes(src, i, width), rows_of(mid, home, tok),
            mid_send.at[n, d - 1], mid_recv.at[n, d - 1], (per * i + core, z),
        )

    def plane_wait(n, src, mid, d):
        j = around(home, -d)
        return remote(
            lanes(src, 0, width), rows_of(mid, j, tok),
            mid_send.at[n, d - 1], mid_recv.at[n, d - 1], (per * j + core, z),
        )

    def forward(n, src, mid, dst, d, act):
        j = around(home, -d)
        piece = lanes(src, home, width) if d == 0 else rows_of(mid, j, tok)
        here = rows_of(dst, z, tok)

        @pl.when(j == z)
        def _():
            act(pltpu.make_async_copy(piece, here, local.at[n]), False)

        @pl.when(j != z)
        def _():
            act(remote(piece, here, tok_send.at[n, d], tok_recv.at[n, z], (e, j)), True)

    def begin(copy, away):
        copy.start()

    def finish(copy, away):
        if away:
            copy.wait_send()
        else:
            copy.wait()

    def token_wait(n, src, dst, t):
        origin = around(z, -t)
        return remote(
            lanes(src, 0, width), rows_of(dst, origin, tok),
            tok_send.at[n, 0], tok_recv.at[n, origin], (e, origin),
        )

    def cell_copy(n, src, dst, j):
        target = lax.rem(e + j, enc)
        return remote(
            lanes(src, slot(target), width), rows_of(dst, e, cells),
            cell_send.at[n, j - 1], cell_recv.at[n, j - 1], (target, z),
        )

    def cell_wait(n, src, dst, j):
        origin = lax.rem(e - j + enc, enc)
        return remote(
            lanes(src, 0, width), rows_of(dst, origin, cells),
            cell_send.at[n, j - 1], cell_recv.at[n, j - 1], (origin, z),
        )

    def cell_own(n, src, dst):
        return pltpu.make_async_copy(
            lanes(src, slot(e), width), rows_of(dst, e, cells), local.at[2 + n]
        )

    def bias_copy(j):
        return remote(
            bias, lanes(bias_all, z, tok), bias_send.at[j - 1], bias_recv.at[j - 1],
            (e, around(z, j)),
        )

    def bias_wait(j):
        origin = around(z, -j)
        return remote(
            bias, lanes(bias_all, origin, tok), bias_send.at[j - 1], bias_recv.at[j - 1],
            (e, origin),
        )

    bias_own = pltpu.make_async_copy(bias, lanes(bias_all, z, tok), local.at[4])
    staged = ((0, q, q_mid, q_all), (1, g, g_mid, g_all))
    celled = ((0, k, k_all), (1, v, v_all))
    for n, src, mid, dst in staged:
        for d in range(1, dec):
            plane_copy(n, src, mid, d).start()
        forward(n, src, mid, dst, 0, begin)
    for j in range(1, dec):
        bias_copy(j).start()
    bias_own.start()
    for n, src, dst in celled:
        for j in range(1, enc):
            cell_copy(n, src, dst, j).start()
        cell_own(n, src, dst).start()
    for n, src, mid, dst in staged:
        for d in range(1, dec):
            plane_wait(n, src, mid, d).wait_recv()
            forward(n, src, mid, dst, d, begin)
    for n, src, mid, dst in staged:
        for d in range(1, dec):
            plane_copy(n, src, mid, d).wait_send()
            token_wait(n, src, dst, d).wait_recv()
        for d in range(dec):
            forward(n, src, mid, dst, d, finish)
    for n, src, dst in celled:
        for j in range(1, enc):
            cell_copy(n, src, dst, j).wait_send()
            cell_wait(n, src, dst, j).wait_recv()
        cell_own(n, src, dst).wait()
    for j in range(1, dec):
        bias_copy(j).wait_send()
        bias_wait(j).wait_recv()
    bias_own.wait()


def gather_kernel(
    *refs
):
    enc, dec = lax.axis_size("enc"), lax.axis_size("dec")
    per = enc // dec
    e, z = lax.axis_index("enc"), lax.axis_index("dec")
    t0, t1, c0, c1, o0, o1, d0, d1, tok_send, tok_recv, cell_send, cell_recv, local = refs
    width = t0.shape[1]
    tok, cells = o0.shape[0], d0.shape[0]
    home, core = e // per, lax.rem(e, per)
    slot = lambda x: lax.rem(x, per) * dec + x // per
    greet_all()

    def token_copy(n, src, dst, i):
        return remote(
            rows_of(src, i, tok), lanes(dst, home, width),
            tok_send.at[n, i], tok_recv.at[n, home], (per * z + core, i),
        )

    def token_wait(n, src, dst, i):
        return remote(
            rows_of(src, 0, tok), lanes(dst, i, width),
            tok_send.at[n, 0], tok_recv.at[n, i], (e, z),
        )

    def token_own(n, src, dst):
        return pltpu.make_async_copy(rows_of(src, z, tok), lanes(dst, home, width), local.at[n])

    def cell_copy(n, src, dst, j):
        target = lax.rem(e + j, enc)
        return remote(
            rows_of(src, target, cells), lanes(dst, slot(e), width),
            cell_send.at[n, j - 1], cell_recv.at[n, j - 1], (target, z),
        )

    def cell_wait(n, src, dst, j):
        origin = lax.rem(e - j + enc, enc)
        return remote(
            rows_of(src, 0, cells), lanes(dst, slot(origin), width),
            cell_send.at[n, j - 1], cell_recv.at[n, j - 1], (origin, z),
        )

    def cell_own(n, src, dst):
        return pltpu.make_async_copy(
            rows_of(src, e, cells), lanes(dst, slot(e), width), local.at[2 + n]
        )

    staged = ((0, t0, o0, c0, d0), (1, t1, o1, c1, d1))
    for n, ts, td, cs, cd in staged:
        for i in range(dec):
            mine = (home == z) & (z == i)
            pl.when(jnp.logical_not(mine))(lambda: token_copy(n, ts, td, i).start())
        pl.when(home == z)(lambda: token_own(n, ts, td).start())
        for j in range(1, enc):
            cell_copy(n, cs, cd, j).start()
        cell_own(n, cs, cd).start()
    for n, ts, td, cs, cd in staged:
        for i in range(dec):
            mine = (home == z) & (z == i)
            pl.when(jnp.logical_not(mine))(lambda: token_copy(n, ts, td, i).wait_send())
            pl.when(jnp.logical_not(mine))(lambda: token_wait(n, ts, td, i).wait_recv())
        pl.when(home == z)(lambda: token_own(n, ts, td).wait())
        for j in range(1, enc):
            cell_copy(n, cs, cd, j).wait_send()
            cell_wait(n, cs, cd, j).wait_recv()
        cell_own(n, cs, cd).wait()


def scatter(q, k, bias, g, v):
    enc, dec = lax.axis_size("enc"), lax.axis_size("dec")
    width = k.shape[1] // (enc * dec)
    bf = jnp.bfloat16
    dma = pltpu.SemaphoreType.DMA
    tokens = jax.ShapeDtypeStruct((dec * q.shape[0], width), bf)
    cells = jax.ShapeDtypeStruct((enc * k.shape[0], width), bf)
    return pl.pallas_call(
        scatter_kernel,
        out_shape=(
            tokens, cells, jax.ShapeDtypeStruct((bias.shape[0], dec * bias.shape[1]), bf),
            tokens, cells, tokens, tokens,
        ),
        in_specs=[pl.BlockSpec(memory_space=pl.ANY)] * 5,
        out_specs=[pl.BlockSpec(memory_space=pl.ANY)] * 7,
        scratch_shapes=[
            dma((2, dec - 1)), dma((2, dec - 1)),
            dma((2, dec)), dma((2, dec)), dma((2, enc - 1)), dma((2, enc - 1)),
            dma((dec - 1,)), dma((dec - 1,)), dma((5,)),
        ],
        compiler_params=pltpu.CompilerParams(collective_id=0, has_side_effects=True),
        name="scatter_in",
    )(q, k, bias, g, v)[:5]


def gather(ctx, dq, dk, dv, tok, cells):
    enc, dec = lax.axis_size("enc"), lax.axis_size("dec")
    width = ctx.shape[1]
    bf = jnp.bfloat16
    dma = pltpu.SemaphoreType.DMA
    token_out = jax.ShapeDtypeStruct((tok, dec * width), bf)
    cell_out = jax.ShapeDtypeStruct((cells, enc * width), bf)
    return pl.pallas_call(
        gather_kernel,
        out_shape=(token_out, token_out, cell_out, cell_out),
        in_specs=[pl.BlockSpec(memory_space=pl.ANY)] * 4,
        out_specs=[pl.BlockSpec(memory_space=pl.ANY)] * 4,
        scratch_shapes=[
            dma((2, dec)), dma((2, dec)), dma((2, enc - 1)), dma((2, enc - 1)), dma((4,)),
        ],
        compiler_params=pltpu.CompilerParams(collective_id=1, has_side_effects=True),
        name="gather_out",
    )(ctx, dq, dk, dv)


def shared_head(q, g, k, v, bias, per, dec):
    share = DH // q.shape[1]
    mates = [
        [per * (j + i) + c for i in range(share)] for c in range(per) for j in range(0, dec, share)
    ]
    place = lax.rem(lax.axis_index("enc") // per, share)
    rows = q.shape[0] // share

    def to_head(x):
        return lax.all_to_all(x, "enc", 0, 1, axis_index_groups=mates, tiled=True)

    def from_head(x):
        return lax.all_to_all(x, "enc", 1, 0, axis_index_groups=mates, tiled=True)

    def widen(x):
        return lax.all_gather(x, "enc", axis=1, axis_index_groups=mates, tiled=True)

    def add_up(x):
        total = lax.psum_scatter(
            x, "enc", scatter_dimension=1, axis_index_groups=mates, tiled=True
        )
        return total.astype(jnp.bfloat16)

    bias = lax.dynamic_slice_in_dim(bias, place * rows, rows, 1)
    ctx, dq, dk, dv = attention(to_head(q), to_head(g), widen(k), widen(v), bias, jnp.float32)
    return from_head(ctx), from_head(dq), add_up(dk), add_up(dv)


def body(queries, out_grad, memory_keys, memory_values, ref_blocks, ref_counts):
    enc, dec = lax.axis_size("enc"), lax.axis_size("dec")
    per = enc // dec
    tok, tok_width = queries.shape
    own_cells, full = memory_keys.shape
    width = full // (enc * dec)
    groups = [[per * k + c for k in range(dec)] for c in range(per)]

    def token_in(x):
        x = x.reshape(tok, dec, width).transpose(1, 0, 2)
        x = lax.all_to_all(x, "enc", 0, 0, axis_index_groups=groups)
        return lax.all_to_all(x, "dec", 0, 0).reshape(dec * tok, width)

    def token_out(x):
        x = lax.all_to_all(x.reshape(dec, tok, width), "dec", 0, 0)
        x = lax.all_to_all(x, "enc", 0, 0, axis_index_groups=groups)
        return x.transpose(1, 0, 2).reshape(tok, tok_width)

    def cell_in(x):
        x = lax.dynamic_slice_in_dim(x, lax.axis_index("dec") * (full // dec), full // dec, 1)
        x = x.reshape(own_cells, per, dec, width).transpose(2, 1, 0, 3)
        x = lax.all_to_all(x.reshape(enc, own_cells, width), "enc", 0, 0)
        return x.reshape(enc * own_cells, width)

    def cell_out(x):
        x = lax.all_to_all(x.reshape(enc, own_cells, width), "enc", 0, 0)
        x = x.reshape(dec, per, own_cells, width).transpose(2, 1, 0, 3)
        return x.reshape(own_cells, full // dec)

    bias = hidden_blocks(ref_blocks, ref_counts, enc * own_cells // BLOCK)
    if width % LANES == 0:
        q, k, bias, g, v = scatter(queries, memory_keys, bias, out_grad, memory_values)
        return gather(*attention(q, g, k, v, bias), tok, own_cells)
    bias = lax.all_gather(bias, "dec", axis=1, tiled=True)
    q, g, k, v = token_in(queries), token_in(out_grad), cell_in(memory_keys), cell_in(memory_values)
    if width >= DH:
        ctx, dq, dk, dv = attention(q, g, k, v, bias)
    else:
        ctx, dq, dk, dv = shared_head(q, g, k, v, bias, per, dec)
    return token_out(ctx), token_out(dq), cell_out(dk), cell_out(dv)


def solution(mesh):
    in_specs = (
        P("dec", "enc"),
        P("dec", "enc"),
        P("enc", None),
        P("enc", None),
        P("dec", None),
        P("dec"),
    )
    out_specs = (P("dec", "enc"), P("dec", "enc"), P("enc", "dec"), P("enc", "dec"))
    return jax.shard_map(body, mesh=mesh, in_specs=in_specs, out_specs=out_specs, check_vma=False)
```
